32 devices in a mesh: groups: 2 (over y), row: 4 (over z), col: 2 (over x), mp: 2 (over core).
Axes of the slice: x: 2, y: 2, z: 4, core: 2. Of those that a mesh axis runs over, the one named last changes fastest.
Arguments:
- queries: bfloat16 [2, 2048, 5120], P('mp', ('groups', 'row'), 'col'), parts along dimension 1, may hold values from -6 to 6
- keys: bfloat16 [2, 2048, 1024], P('mp', ('groups', 'row'), 'col'), parts along dimension 1, may hold values from -6 to 6
- values: bfloat16 [2, 2048, 1024], P('mp', ('groups', 'row'), 'col'), parts along dimension 1, may hold values from -6 to 6
- lengths: int32 [4], P('groups'), parts along dimension 0, may hold values from 1 to 768, 1024 in all
Outputs:
- outputs: bfloat16 [2, 2048, 5120], P('mp', ('groups', 'row'), 'col'), parts along dimension 1
- gap: float32 [40, 2048], P(('col', 'mp'), ('groups', 'row')), parts along dimension 1
The draws below stay inside these ranges and needn't reach their ends.
There are 2 independent parts, one for each index of `groups`. The reference program is written for one: setup_inputs(seed, part) draws one part's arguments, and reference() takes and returns one part's arrays. A program takes and returns all parts, laid end to end along the dimension named above; each array names one. Nothing has to cross between parts.
Inputs may be any that keep to these rules, and one draw needn't show every extreme that they name: The 2 lengths sum to 1024; one rollout is exactly 768 tokens long.
All inputs are finite; a program needn't handle non-finite values.
Results may differ from the reference program's by a relative error of at most 0.011.
Values may be sent and summed in bfloat16 or wider, within the bound.
A program may use at most 64 MiB of HBM per device.

```python
import math
import jax
import jax.numpy as jnp
import numpy as np
from jax import lax

HEADS = 40
KV_HEADS = 8
HEAD_DIM = 128
TOK_DEV = 256
GROUP = 5
TOKENS = 1024
NSEQ = 2
MAXLEN = 768
N_ROW = 4


def base_rows(key, width):
    return jnp.clip(jax.random.normal(jax.random.fold_in(key, 23), (2, TOKENS, width)), -6.0, 6.0)


def draw_keys(key, part):
    width = KV_HEADS * HEAD_DIM
    draws = base_rows(jax.random.fold_in(key, 37), width)
    return draws.astype(jnp.bfloat16)


def draw_queries(key, part):
    width = HEADS * HEAD_DIM
    draws = base_rows(jax.random.fold_in(key, 31), width)
    return draws.astype(jnp.bfloat16)


def level_of(key, dims, split, low, high):
    level = 1.0
    for position, parts in split:
        steps = jax.random.uniform(jax.random.fold_in(jax.random.fold_in(key, 6), position), (parts,), jnp.float32, low / len(split), high / len(split))
        level = level * jnp.repeat(jnp.exp(steps), dims[position] // parts).reshape((-1,) + (1,) * (len(dims) - 1 - position))
    return level


def length_profile(number_of, total, bound, skew):
    weights = [(1 << 20) // math.isqrt(standing ** skew) + 1 for standing in range(2, number_of + 1)]
    surplus, counts = total - bound - (number_of - 1), [1] * (number_of - 1)
    while surplus > 0:
        candidates = [i for i in range(number_of - 1) if counts[i] < bound]
        pool, left = sum([weights[i] for i in candidates]), surplus
        for i in candidates:
            addition = min(bound - counts[i], max(1, left * weights[i] // pool), surplus)
            counts[i] = counts[i] + addition
            surplus = surplus - addition
    return np.array([bound] + counts)


def ragged(rng, number_of, total, most, slope):
    if number_of == 2:
        one = jax.random.randint(rng, (), max(1, total - most), min(most, total - 1) + 1)
        return jnp.stack([one, total - one])
    tallies = jnp.asarray(length_profile(number_of, total, most, slope), jnp.int32)
    couples = (number_of - 1) // 2
    giver, sink = tallies[1:1 + 2 * couples:2], tallies[2:2 + 2 * couples:2]
    slack = jnp.minimum(giver - 1, most - sink)
    shifted = jax.random.randint(jax.random.fold_in(rng, 1), (couples,), 0, 1 << 20) % (slack + 1)
    tallies = tallies.at[1:1 + 2 * couples:2].set(giver - shifted).at[2:2 + 2 * couples:2].set(sink + shifted)
    return tallies[jax.random.permutation(jax.random.fold_in(rng, 2), number_of)]


def gaussian(rng, dims, scale, most, pieces=(), kind=jnp.bfloat16):
    result = scale * jax.random.normal(rng, dims, jnp.float32)
    if pieces:
        result = result * level_of(rng, dims, pieces, -0.22, 0.18)
    return jnp.clip(result, -most, most).astype(kind)


def setup_inputs(seed: int = 0, part: int = 0) -> dict:
    seeds = jax.random.split(jax.random.key(seed), 5)
    part_splits = jax.random.split(jax.random.fold_in(seeds[4], part), 5)
    queries = draw_queries(jax.random.fold_in(jax.random.fold_in(seeds[4], part), 71), part)
    keys = draw_keys(jax.random.fold_in(jax.random.fold_in(seeds[4], part), 71), part)
    values = gaussian(part_splits[2], (2, TOKENS, KV_HEADS * HEAD_DIM), 1.0, 6.0, ((0, 2), (1, 4), (2, 2)))
    lengths = ragged(part_splits[3], NSEQ, TOKENS, MAXLEN, 2).astype(jnp.int32)
    return {"queries": queries, "keys": keys, "values": values, "lengths": lengths}


def rollout_begin(lengths, positions):
    finish = jnp.cumsum(lengths).astype(jnp.int32)
    return lax.optimization_barrier(jnp.sum(jnp.where(finish[None, :] <= positions[:, None], lengths[None, :], 0), axis=1)).astype(jnp.int32)

def attend(queries, keys, values, begin_at):
    padded_keys = jnp.pad(keys, ((MAXLEN, 0), (0, 0)))
    padded_values = jnp.pad(values, ((MAXLEN, 0), (0, 0)))
    window = MAXLEN + TOK_DEV
    factor = 1.0 / math.sqrt(HEAD_DIM)

    def one_block(block_id):
        offset = (block_id * TOK_DEV).astype(jnp.int32)
        query_rows = lax.dynamic_slice_in_dim(queries, offset, TOK_DEV, 0).astype(jnp.float32).reshape(TOK_DEV, KV_HEADS, GROUP, HEAD_DIM)
        key_rows = lax.dynamic_slice_in_dim(padded_keys, offset, window, 0).astype(jnp.float32).reshape(window, KV_HEADS, HEAD_DIM)
        value_rows = lax.dynamic_slice_in_dim(padded_values, offset, window, 0).astype(jnp.float32).reshape(window, KV_HEADS, HEAD_DIM)
        scores = jnp.einsum('tkgd,nkd->kgtn', query_rows, key_rows, precision=lax.Precision.HIGHEST) * factor
        query_pos = offset + jnp.arange(TOK_DEV, dtype=jnp.int32)
        key_pos = offset - MAXLEN + jnp.arange(window, dtype=jnp.int32)
        lowest = lax.dynamic_slice_in_dim(begin_at, offset, TOK_DEV, 0)
        allowed = (key_pos[None, :] >= lowest[:, None]) & (key_pos[None, :] <= query_pos[:, None])
        masked = jnp.where(allowed, scores, -jnp.inf)
        highest = lax.optimization_barrier(jnp.max(masked, axis=-1, keepdims=True))
        weights = jnp.where(allowed, jnp.exp(masked - highest), 0.0)
        summed = lax.optimization_barrier(jnp.sum(weights, axis=-1))
        rounded = lax.optimization_barrier(weights.astype(jnp.bfloat16))
        mass = rounded.astype(jnp.float32)
        mixed = jnp.einsum('kgtn,nkd->kgtd', mass, value_rows, precision=lax.Precision.HIGHEST) / summed[..., None]
        return jnp.transpose(mixed, (2, 0, 1, 3)).reshape(TOK_DEV, HEADS * HEAD_DIM).astype(jnp.bfloat16)
    blocks = lax.map(one_block, jnp.arange(N_ROW, dtype=jnp.int32))
    return blocks.reshape(TOKENS, HEADS * HEAD_DIM)

def reference(queries, keys, values, lengths):
    positions = jnp.arange(TOKENS, dtype=jnp.int32)
    begin_at = rollout_begin(lengths.astype(jnp.int32), positions)
    policy = attend(queries[0], keys[0], values[0], begin_at)
    anchor = attend(queries[1], keys[1], values[1], begin_at)
    outputs = jnp.stack([policy, anchor])
    first = policy.astype(jnp.float32).reshape(TOKENS, HEADS, HEAD_DIM)
    second = anchor.astype(jnp.float32).reshape(TOKENS, HEADS, HEAD_DIM)
    difference = first - second
    scale_sum = lax.optimization_barrier(jnp.mean(first * first, axis=-1)) + 1e-06
    gap = jnp.transpose(lax.optimization_barrier(jnp.mean(difference * difference, axis=-1)) / scale_sum)
    return (outputs, gap)
```

```python
import functools
import math

import jax
import jax.numpy as jnp
from jax import lax
from jax.experimental import pallas as pl
from jax.experimental.pallas import tpu as pltpu
from jax.sharding import PartitionSpec as P

HEADS = 40
KV_HEADS = 8
HEAD_DIM = 128


def from_behind(block, axis, distance):
    devices = range(lax.axis_size(axis))
    route = [(i - distance, i) for i in devices if i - distance in devices]
    return lax.ppermute(block, axis, route)


def swapped(block, axis, distance):
    count = lax.axis_size(axis)
    route = []
    for low in range(count):
        high = low | 1 << distance
        if high != low and high < count:
            route += [(low, high), (high, low)]
    return lax.ppermute(block, axis, route)


def relative_gap(first, second, tokens_here, heads_count):
    first = first.astype(jnp.float32).reshape(tokens_here, heads_count, HEAD_DIM)
    second = second.astype(jnp.float32).reshape(tokens_here, heads_count, HEAD_DIM)
    difference = first - second
    scale_sum = jnp.mean(first * first, axis=-1) + 1e-06
    return jnp.transpose(jnp.mean(difference * difference, axis=-1) / scale_sum)


def per_device(queries, keys, values, lengths):
    tokens_here = queries.shape[1]
    width_here = keys.shape[2]
    kv_local = width_here // HEAD_DIM
    group_size = HEADS // KV_HEADS
    heads_local = kv_local * group_size
    factor = 1.0 / math.sqrt(HEAD_DIM)
    row_pos = lax.axis_index("row")
    first_pos = row_pos * tokens_here
    query_pos = first_pos + jnp.arange(tokens_here, dtype=jnp.int32)
    finish = jnp.cumsum(lengths)
    begin_at = jnp.sum(
        jnp.where(finish[None, :] <= query_pos[:, None], lengths[None, :], 0), axis=1
    )
    lowest = begin_at[0]
    highest = first_pos + tokens_here - 1
    query_rows = queries[0].reshape(tokens_here, kv_local, group_size, HEAD_DIM)

    def update(running, stacked, offset):
        best, summed, accum = running
        amount = stacked.shape[1]
        key_rows = stacked[0].reshape(amount, kv_local, HEAD_DIM)
        value_rows = stacked[1].reshape(amount, kv_local, HEAD_DIM)
        scores = (
            jnp.einsum("tkgd,nkd->kgtn", query_rows, key_rows, preferred_element_type=jnp.float32)
            * factor
        )
        key_pos = offset + jnp.arange(amount, dtype=jnp.int32)
        allowed = (key_pos[None, :] >= begin_at[:, None]) & (key_pos[None, :] <= query_pos[:, None])
        masked = jnp.where(allowed, scores, -jnp.inf)
        fresh_best = jnp.maximum(best, jnp.max(masked, axis=-1))
        weights = jnp.where(allowed, jnp.exp(masked - fresh_best[..., None]), 0.0)
        shrink = jnp.exp(best - fresh_best)
        summed = summed * shrink + jnp.sum(weights, axis=-1)
        accum = accum * shrink[..., None] + jnp.einsum(
            "kgtn,nkd->kgtd",
            weights.astype(jnp.bfloat16),
            value_rows,
            preferred_element_type=jnp.float32,
        )
        return (fresh_best, summed, accum)

    def absorb(running, stacked, offset):
        amount = stacked.shape[1]
        needed = (offset + amount > lowest) & (offset <= highest)
        return lax.cond(
            needed, lambda inner: update(inner, stacked, offset), lambda inner: inner, running
        )

    start_state = (
        jnp.full((kv_local, group_size, tokens_here), -1e30, jnp.float32),
        jnp.zeros((kv_local, group_size, tokens_here), jnp.float32),
        jnp.zeros((kv_local, group_size, tokens_here, HEAD_DIM), jnp.float32),
    )
    paired = jnp.concatenate([keys, values], axis=0)
    reach = lax.axis_size("row") // 2 + 1
    running = absorb(start_state, paired, first_pos)

    def advance(step_id, loop_state):
        inner, moving = loop_state
        moving = from_behind(moving, "row", 1)
        return (absorb(inner, moving, (row_pos - step_id) * tokens_here), moving)

    running, _ = lax.fori_loop(1, reach + 1, advance, (running, paired))
    best, summed, accum = running
    mixed = accum / summed[..., None]
    outputs = (
        jnp.transpose(mixed, (2, 0, 1, 3))
        .reshape(tokens_here, heads_local * HEAD_DIM)
        .astype(jnp.bfloat16)[None]
    )
    half_heads = heads_local // 2
    partner = swapped(outputs, "mp", 0)
    model_pos = lax.axis_index("mp")
    is_policy = model_pos == 0
    policy = jnp.where(is_policy, outputs[0], partner[0])
    anchor = jnp.where(is_policy, partner[0], outputs[0])
    column_at = model_pos * half_heads * HEAD_DIM
    policy_part = lax.dynamic_slice_in_dim(policy, column_at, half_heads * HEAD_DIM, 1)
    anchor_part = lax.dynamic_slice_in_dim(anchor, column_at, half_heads * HEAD_DIM, 1)
    gap = relative_gap(policy_part, anchor_part, tokens_here, half_heads)
    return (outputs, gap)


MESH = pl.DeviceIdType.MESH
DROP = -1e30


def kernel(sizes, lens, q_in, k_in, v_in, o_out, gap_out, q_buf, kv_own, kv_prev, kv_far, kv_pick,
           o_buf, other, bias, gap_num, gap_den, q_sem, kv_sem, o_sem, prev_send, prev_recv, far_send,
           far_recv, mp_send, mp_recv):
    rows, tokens, kv_local, group = sizes
    wide = group * HEAD_DIM
    half = kv_local // 2
    factor = math.log2(math.e) / math.sqrt(HEAD_DIM)
    row = lax.axis_index("row")
    mp = lax.axis_index("mp")
    after = lax.rem(row + 1, rows)
    before = lax.rem(row + rows - 1, rows)

    def head_of(i):
        return lax.rem(i + half * (1 - mp), kv_local)

    def cols(i):
        return pl.ds(pl.multiple_of(head_of(i) * HEAD_DIM, HEAD_DIM), HEAD_DIM)

    def wide_cols(i):
        return pl.ds(pl.multiple_of(head_of(i) * wide, HEAD_DIM), wide)

    def local_kv(i, n):
        src = (k_in, v_in)[n]
        return pltpu.make_async_copy(src.at[0, :, cols(i)], kv_own.at[i, n], kv_sem.at[i, n])

    def local_q(i):
        return pltpu.make_async_copy(
            q_in.at[0, :, wide_cols(i)], q_buf.at[:, wide_cols(i)], q_sem.at[i]
        )

    def local_o(i):
        return pltpu.make_async_copy(
            o_buf.at[:, wide_cols(i)], o_out.at[0, :, wide_cols(i)], o_sem.at[i]
        )

    def to_prev(i, n):
        src = (k_in, v_in)[n]
        return pltpu.make_async_remote_copy(
            src_ref=src.at[0, :, cols(i)], dst_ref=kv_prev.at[i, n],
            send_sem=prev_send.at[i, n], recv_sem=prev_recv.at[i, n],
            device_id={"row": after}, device_id_type=MESH,
        )

    def to_far(i, n, src):
        return pltpu.make_async_remote_copy(
            src_ref=src, dst_ref=kv_far.at[i, n],
            send_sem=far_send.at[i, n], recv_sem=far_recv.at[i, n],
            device_id={"row": before}, device_id_type=MESH,
        )

    def far_own(i, n):
        return to_far(i, n, (k_in, v_in)[n].at[0, :, cols(i)])

    def to_mate(i):
        return pltpu.make_async_remote_copy(
            src_ref=o_buf.at[:, wide_cols(i)], dst_ref=other.at[i],
            send_sem=mp_send.at[i], recv_sem=mp_recv.at[i],
            device_id={"mp": 1 - mp}, device_id_type=MESH,
        )

    for i in range(kv_local):
        for n in range(2):
            local_kv(i, n).start()
        local_q(i).start()
    barrier = pltpu.get_barrier_semaphore()
    for neighbour in (after, before):
        pl.semaphore_signal(barrier, inc=1, device_id={"row": neighbour}, device_id_type=MESH)
    pl.semaphore_signal(barrier, inc=1, device_id={"mp": 1 - mp}, device_id_type=MESH)
    pl.semaphore_wait(barrier, 3)

    for i in range(kv_local):
        for n in range(2):
            @pl.when(row == 1)
            def _():
                far_own(i, n).start()

            @pl.when(row < rows - 1)
            def _():
                to_prev(i, n).start()

    first, second = lens[0], lens[1]

    def begin_of(block):
        at = block * tokens
        return jnp.where(first <= at, first, 0) + jnp.where(first + second <= at, second, 0)

    qi = lax.broadcasted_iota(jnp.int32, (tokens, tokens), 0) + row * tokens
    ki = lax.broadcasted_iota(jnp.int32, (tokens, tokens), 1) + row * tokens
    begin = jnp.where(first <= qi, first, 0) + jnp.where(first + second <= qi, second, 0)
    bias[0] = jnp.where((ki >= begin) & (ki <= qi), 0.0, DROP)
    bias[1] = jnp.where(ki - tokens >= begin, 0.0, DROP)
    bias[2] = jnp.where(ki - 2 * tokens >= begin, 0.0, DROP)

    @pl.when(row == 1)
    def _():
        kv_far[...] = jnp.zeros_like(kv_far)

    @pl.when(row == 0)
    def _():
        last_needs = jnp.where(begin_of(rows - 1) < (rows - 2) * tokens, 1.0, 0.0)
        for i in range(kv_local):
            for n in range(2):
                local_kv(i, n).wait()
                to_far(i, n, kv_pick.at[i, n]).wait_recv()
                flag = jnp.broadcast_to(last_needs, (tokens, HEAD_DIM))
                kv_pick[i, n] = jnp.where(
                    flag > 0.5,
                    kv_far[i, n].astype(jnp.float32),
                    kv_own[i, n].astype(jnp.float32),
                ).astype(jnp.bfloat16)
                to_far(i, n, kv_pick.at[i, n]).start()

    def dot_t(a, b):
        return lax.dot_general(a, b, (((1,), (1,)), ((), ())), preferred_element_type=jnp.float32)

    def dot(a, b):
        return jnp.dot(a.astype(jnp.bfloat16), b, preferred_element_type=jnp.float32)

    def head_cols(i, g):
        at = head_of(i) * wide + g * HEAD_DIM
        return pl.ds(pl.multiple_of(at, HEAD_DIM), HEAD_DIM)

    def one_head(i, g, full):
        at = head_cols(i, g)
        q = q_buf[:, at]
        near = dot_t(q, kv_own[i, 0]) + bias[0]
        top = jnp.max(near, axis=-1, keepdims=True)
        if full:
            prev = dot_t(q, kv_prev[i, 0]) + bias[1]
            far = dot_t(q, kv_far[i, 0]) + bias[2]
            top = jnp.maximum(top, jnp.max(prev, axis=-1, keepdims=True))
            top = jnp.maximum(top, jnp.max(far, axis=-1, keepdims=True))
        near = jnp.exp2((near - top) * factor)
        total = jnp.sum(near, axis=-1, keepdims=True)
        mixed = dot(near, kv_own[i, 1])
        if full:
            prev = jnp.exp2((prev - top) * factor)
            total += jnp.sum(prev, axis=-1, keepdims=True)
            mixed += dot(prev, kv_prev[i, 1])
            far = jnp.exp2((far - top) * factor)
            total += jnp.sum(far, axis=-1, keepdims=True)
            mixed += dot(far, kv_far[i, 1])
        o_buf[:, at] = (mixed / total).astype(jnp.bfloat16)

    lane = lax.broadcasted_iota(jnp.int32, (tokens, HEAD_DIM), 1)
    gap_num[...] = jnp.zeros_like(gap_num)
    gap_den[...] = jnp.zeros_like(gap_den)

    for i in range(kv_local):
        local_q(i).wait()

        @pl.when(row == 0)
        def _():
            lax.fori_loop(0, group, lambda g, c: (one_head(i, g, False), c)[1], 0)

        @pl.when(row > 0)
        def _():
            for n in range(2):
                local_kv(i, n).wait()
                to_prev(i, n).wait_recv()

            @pl.when(row > 1)
            def _():
                for n in range(2):
                    to_far(i, n, kv_far.at[i, n]).wait_recv()

                    @pl.when(row == rows - 1)
                    def _():
                        to_far(i, n, kv_far.at[i, n]).start()

            for g in range(group):
                one_head(i, g, True)

        local_o(i).start()
        if i < half:
            to_mate(i).start()
        else:
            to_mate(i - half).wait_recv()
            for g in range(group):
                mine = o_buf[:, head_cols(i, g)].astype(jnp.float32)
                theirs = other[i - half, :, g * HEAD_DIM:(g + 1) * HEAD_DIM].astype(jnp.float32)
                policy = jnp.where(mp == 0, mine, theirs)
                apart = mine - theirs
                here = lane == (i - half) * group + g
                gap_num[...] = jnp.where(
                    here, jnp.sum(apart * apart, axis=-1, keepdims=True), gap_num[...]
                )
                gap_den[...] = jnp.where(
                    here, jnp.sum(policy * policy, axis=-1, keepdims=True), gap_den[...]
                )
    num = jnp.transpose(gap_num[...])[: half * group] / HEAD_DIM
    den = jnp.transpose(gap_den[...])[: half * group] / HEAD_DIM
    gap_out[...] = num / (den + 1e-06)

    for i in range(kv_local):
        local_o(i).wait()
        if i < half:
            to_mate(i).wait_send()
        for n in range(2):
            @pl.when(row < rows - 1)
            def _():
                to_prev(i, n).wait_send()

            @pl.when(row == 1)
            def _():
                far_own(i, n).wait_send()

            @pl.when((row == 0) | (row == rows - 1))
            def _():
                to_far(i, n, kv_pick.at[i, n]).wait_send()


def fused(rows, queries, keys, values, lengths):
    tokens = queries.shape[1]
    kv_local = keys.shape[2] // HEAD_DIM
    group = HEADS // KV_HEADS
    width = queries.shape[2]
    half = kv_local // 2
    kv = pltpu.VMEM((kv_local, 2, tokens, HEAD_DIM), jnp.bfloat16)
    dma = pltpu.SemaphoreType.DMA
    return pl.pallas_call(
        functools.partial(kernel, (rows, tokens, kv_local, group)),
        out_shape=(
            jax.ShapeDtypeStruct((1, tokens, width), jnp.bfloat16),
            jax.ShapeDtypeStruct((half * group, tokens), jnp.float32),
        ),
        in_specs=[pl.BlockSpec(memory_space=pltpu.SMEM)] + [pl.BlockSpec(memory_space=pl.ANY)] * 3,
        out_specs=(pl.BlockSpec(memory_space=pl.ANY), pl.BlockSpec(memory_space=pltpu.VMEM)),
        scratch_shapes=[
            pltpu.VMEM((tokens, width), jnp.bfloat16),
            kv, kv, kv, kv,
            pltpu.VMEM((tokens, width), jnp.bfloat16),
            pltpu.VMEM((half, tokens, group * HEAD_DIM), jnp.bfloat16),
            pltpu.VMEM((3, tokens, tokens), jnp.float32),
            pltpu.VMEM((tokens, HEAD_DIM), jnp.float32),
            pltpu.VMEM((tokens, HEAD_DIM), jnp.float32),
            dma((kv_local,)), dma((kv_local, 2)), dma((kv_local,)),
            dma((kv_local, 2)), dma((kv_local, 2)), dma((kv_local, 2)), dma((kv_local, 2)),
            dma((half,)), dma((half,)),
        ],
        compiler_params=pltpu.CompilerParams(
            collective_id=0, has_side_effects=True, vmem_limit_bytes=48 << 20
        ),
    )(lengths, queries, keys, values)


def solution(mesh):
    in_specs = (
        P("mp", ("groups", "row"), "col"),
        P("mp", ("groups", "row"), "col"),
        P("mp", ("groups", "row"), "col"),
        P("groups"),
    )
    out_specs = (P("mp", ("groups", "row"), "col"), P(("col", "mp"), ("groups", "row")))
    rows = mesh.shape["row"]

    def body(queries, keys, values, lengths):
        if lengths.shape[0] == 2 and rows == 4:
            return fused(rows, queries, keys, values, lengths)
        return per_device(queries, keys, values, lengths)

    return jax.shard_map(
        body, mesh=mesh, in_specs=in_specs, out_specs=out_specs, check_vma=False
    )
```

```python
import functools
import math

import jax
import jax.numpy as jnp
from jax import lax
from jax.experimental import pallas as pl
from jax.experimental.pallas import tpu as pltpu
from jax.sharding import PartitionSpec as P

HEADS = 40
KV_HEADS = 8
HEAD_DIM = 128


def from_behind(block, axis, distance):
    devices = range(lax.axis_size(axis))
    route = [(i - distance, i) for i in devices if i - distance in devices]
    return lax.ppermute(block, axis, route)


def swapped(block, axis, distance):
    count = lax.axis_size(axis)
    route = []
    for low in range(count):
        high = low | 1 << distance
        if high != low and high < count:
            route += [(low, high), (high, low)]
    return lax.ppermute(block, axis, route)


def relative_gap(first, second, tokens_here, heads_count):
    first = first.astype(jnp.float32).reshape(tokens_here, heads_count, HEAD_DIM)
    second = second.astype(jnp.float32).reshape(tokens_here, heads_count, HEAD_DIM)
    difference = first - second
    scale_sum = jnp.mean(first * first, axis=-1) + 1e-06
    return jnp.transpose(jnp.mean(difference * difference, axis=-1) / scale_sum)


def per_device(queries, keys, values, lengths):
    tokens_here = queries.shape[1]
    width_here = keys.shape[2]
    kv_local = width_here // HEAD_DIM
    group_size = HEADS // KV_HEADS
    heads_local = kv_local * group_size
    factor = 1.0 / math.sqrt(HEAD_DIM)
    row_pos = lax.axis_index("row")
    first_pos = row_pos * tokens_here
    query_pos = first_pos + jnp.arange(tokens_here, dtype=jnp.int32)
    finish = jnp.cumsum(lengths)
    begin_at = jnp.sum(
        jnp.where(finish[None, :] <= query_pos[:, None], lengths[None, :], 0), axis=1
    )
    lowest = begin_at[0]
    highest = first_pos + tokens_here - 1
    query_rows = queries[0].reshape(tokens_here, kv_local, group_size, HEAD_DIM)

    def update(running, stacked, offset):
        best, summed, accum = running
        amount = stacked.shape[1]
        key_rows = stacked[0].reshape(amount, kv_local, HEAD_DIM)
        value_rows = stacked[1].reshape(amount, kv_local, HEAD_DIM)
        scores = (
            jnp.einsum("tkgd,nkd->kgtn", query_rows, key_rows, preferred_element_type=jnp.float32)
            * factor
        )
        key_pos = offset + jnp.arange(amount, dtype=jnp.int32)
        allowed = (key_pos[None, :] >= begin_at[:, None]) & (key_pos[None, :] <= query_pos[:, None])
        masked = jnp.where(allowed, scores, -jnp.inf)
        fresh_best = jnp.maximum(best, jnp.max(masked, axis=-1))
        weights = jnp.where(allowed, jnp.exp(masked - fresh_best[..., None]), 0.0)
        shrink = jnp.exp(best - fresh_best)
        summed = summed * shrink + jnp.sum(weights, axis=-1)
        accum = accum * shrink[..., None] + jnp.einsum(
            "kgtn,nkd->kgtd",
            weights.astype(jnp.bfloat16),
            value_rows,
            preferred_element_type=jnp.float32,
        )
        return (fresh_best, summed, accum)

    def absorb(running, stacked, offset):
        amount = stacked.shape[1]
        needed = (offset + amount > lowest) & (offset <= highest)
        return lax.cond(
            needed, lambda inner: update(inner, stacked, offset), lambda inner: inner, running
        )

    start_state = (
        jnp.full((kv_local, group_size, tokens_here), -1e30, jnp.float32),
        jnp.zeros((kv_local, group_size, tokens_here), jnp.float32),
        jnp.zeros((kv_local, group_size, tokens_here, HEAD_DIM), jnp.float32),
    )
    paired = jnp.concatenate([keys, values], axis=0)
    reach = lax.axis_size("row") // 2 + 1
    running = absorb(start_state, paired, first_pos)

    def advance(step_id, loop_state):
        inner, moving = loop_state
        moving = from_behind(moving, "row", 1)
        return (absorb(inner, moving, (row_pos - step_id) * tokens_here), moving)

    running, _ = lax.fori_loop(1, reach + 1, advance, (running, paired))
    best, summed, accum = running
    mixed = accum / summed[..., None]
    outputs = (
        jnp.transpose(mixed, (2, 0, 1, 3))
        .reshape(tokens_here, heads_local * HEAD_DIM)
        .astype(jnp.bfloat16)[None]
    )
    half_heads = heads_local // 2
    partner = swapped(outputs, "mp", 0)
    model_pos = lax.axis_index("mp")
    is_policy = model_pos == 0
    policy = jnp.where(is_policy, outputs[0], partner[0])
    anchor = jnp.where(is_policy, partner[0], outputs[0])
    column_at = model_pos * half_heads * HEAD_DIM
    policy_part = lax.dynamic_slice_in_dim(policy, column_at, half_heads * HEAD_DIM, 1)
    anchor_part = lax.dynamic_slice_in_dim(anchor, column_at, half_heads * HEAD_DIM, 1)
    gap = relative_gap(policy_part, anchor_part, tokens_here, half_heads)
    return (outputs, gap)


MESH = pl.DeviceIdType.MESH
DROP = -1e30


def kernel(sizes, lens_in, q_in, k_in, v_in, o_out, gap_out, lens, q_buf, kv_own, kv_prev, kv_far,
           o_buf, other, bias, gap_num, gap_den, tops, totals, mixes, far_mass, lens_sem, q_sem,
           kv_sem, o_sem, prev_send, prev_recv, far_send, far_recv, mp_send, mp_recv):
    rows, tokens, kv_local, group = sizes
    wide = group * HEAD_DIM
    half = kv_local // 2
    factor = math.log2(math.e) / math.sqrt(HEAD_DIM)
    row = lax.axis_index("row")
    mp = lax.axis_index("mp")
    after = lax.rem(row + 1, rows)
    before = lax.rem(row + rows - 1, rows)

    def head_of(i):
        return lax.rem(i + half * (1 - mp), kv_local)

    def cols(i):
        return pl.ds(pl.multiple_of(head_of(i) * HEAD_DIM, HEAD_DIM), HEAD_DIM)

    def wide_cols(i):
        return pl.ds(pl.multiple_of(head_of(i) * wide, HEAD_DIM), wide)

    def local_kv(i, n):
        src = (k_in, v_in)[n]
        return pltpu.make_async_copy(src.at[0, :, cols(i)], kv_own.at[i, n], kv_sem.at[i, n])

    def local_q(i):
        return pltpu.make_async_copy(
            q_in.at[0, :, wide_cols(i)], q_buf.at[:, wide_cols(i)], q_sem.at[i]
        )

    def local_o(i):
        return pltpu.make_async_copy(
            o_buf.at[:, wide_cols(i)], o_out.at[0, :, wide_cols(i)], o_sem.at[i]
        )

    def to_prev(i, n):
        src = (k_in, v_in)[n]
        return pltpu.make_async_remote_copy(
            src_ref=src.at[0, :, cols(i)], dst_ref=kv_prev.at[i, n],
            send_sem=prev_send.at[i, n], recv_sem=prev_recv.at[i, n],
            device_id={"row": after}, device_id_type=MESH,
        )

    def to_far(i, n):
        return pltpu.make_async_remote_copy(
            src_ref=kv_prev.at[i, n], dst_ref=kv_far.at[i, n],
            send_sem=far_send.at[i, n], recv_sem=far_recv.at[i, n],
            device_id={"row": after}, device_id_type=MESH,
        )

    def to_mate(i):
        return pltpu.make_async_remote_copy(
            src_ref=o_buf.at[:, wide_cols(i)], dst_ref=other.at[i],
            send_sem=mp_send.at[i], recv_sem=mp_recv.at[i],
            device_id={"mp": 1 - mp}, device_id_type=MESH,
        )

    lens_copy = pltpu.make_async_copy(lens_in, lens, lens_sem)
    lens_copy.start()
    for i in range(kv_local):
        for n in range(2):
            local_kv(i, n).start()
        local_q(i).start()
    barrier = pltpu.get_barrier_semaphore()
    for neighbour in (after, before):
        pl.semaphore_signal(barrier, inc=1, device_id={"row": neighbour}, device_id_type=MESH)
    pl.semaphore_signal(barrier, inc=1, device_id={"mp": 1 - mp}, device_id_type=MESH)
    pl.semaphore_wait(barrier, 3)

    @pl.when(row < rows - 1)
    def _():
        for i in range(kv_local):
            for n in range(2):
                to_prev(i, n).start()

    @pl.when(row == 0)
    def _():
        kv_prev[...] = jnp.zeros_like(kv_prev)

    @pl.when(row < 2)
    def _():
        kv_far[...] = jnp.zeros_like(kv_far)

    lens_copy.wait()
    first, second = lens[0], lens[1]
    qi = lax.broadcasted_iota(jnp.int32, (tokens, tokens), 0) + row * tokens
    ki = lax.broadcasted_iota(jnp.int32, (tokens, tokens), 1) + row * tokens
    begin = jnp.where(first <= qi, first, 0) + jnp.where(first + second <= qi, second, 0)
    bias[0] = jnp.where((ki >= begin) & (ki <= qi), 0.0, DROP)
    bias[1] = jnp.where(ki - tokens >= begin, 0.0, DROP)
    bias[2] = jnp.where(ki - 2 * tokens >= begin, 0.0, DROP)
    gap_num[...] = jnp.zeros_like(gap_num)
    gap_den[...] = jnp.zeros_like(gap_den)
    for i in range(kv_local):
        local_q(i).wait()
        for n in range(2):
            local_kv(i, n).wait()

    @pl.when(row > 0)
    def _():
        for i in range(kv_local):
            for n in range(2):
                to_prev(i, n).wait_recv()

                @pl.when(row < rows - 1)
                def _():
                    to_far(i, n).start()

    def dot_t(a, b):
        return lax.dot_general(a, b, (((1,), (1,)), ((), ())), preferred_element_type=jnp.float32)

    def dot(a, b):
        return jnp.dot(a.astype(jnp.bfloat16), b, preferred_element_type=jnp.float32)

    def head_cols(i, g):
        at = head_of(i) * wide + g * HEAD_DIM
        return pl.ds(pl.multiple_of(at, HEAD_DIM), HEAD_DIM)

    def near_part(i, g):
        q = q_buf[:, head_cols(i, g)]
        own = dot_t(q, kv_own[i, 0]) + bias[0]
        prev = dot_t(q, kv_prev[i, 0]) + bias[1]
        top = jnp.maximum(
            jnp.max(own, axis=-1, keepdims=True), jnp.max(prev, axis=-1, keepdims=True)
        )
        own = jnp.exp2((own - top) * factor)
        prev = jnp.exp2((prev - top) * factor)
        total = jnp.sum(own, axis=-1, keepdims=True) + jnp.sum(prev, axis=-1, keepdims=True)
        tops[g] = jnp.broadcast_to(top, (tokens, HEAD_DIM))
        totals[g] = jnp.broadcast_to(total, (tokens, HEAD_DIM))
        mixes[g] = dot(own, kv_own[i, 1]) + dot(prev, kv_prev[i, 1])

    def far_part(i, g):
        q = q_buf[:, head_cols(i, g)]
        far = dot_t(q, kv_far[i, 0]) + bias[2]
        old = tops[g][:, :1]
        top = jnp.maximum(old, jnp.max(far, axis=-1, keepdims=True))
        far = jnp.exp2((far - top) * factor)
        shrink = jnp.exp2((old - top) * factor)
        total = totals[g][:, :1] * shrink + jnp.sum(far, axis=-1, keepdims=True)
        totals[g] = jnp.broadcast_to(1.0 / total, (tokens, HEAD_DIM))
        mixes[g] = mixes[g] * shrink
        far_mass[g] = far.astype(jnp.bfloat16)

    def last_part(i, g):
        mixed = mixes[g] + dot(far_mass[g], kv_far[i, 1])
        o_buf[:, head_cols(i, g)] = (mixed * totals[g]).astype(jnp.bfloat16)

    def one_head(i, g):
        at = head_cols(i, g)
        q = q_buf[:, at]
        near = dot_t(q, kv_own[i, 0]) + bias[0]
        prev = dot_t(q, kv_prev[i, 0]) + bias[1]
        far = dot_t(q, kv_far[i, 0]) + bias[2]
        top = jnp.maximum(
            jnp.max(near, axis=-1, keepdims=True), jnp.max(prev, axis=-1, keepdims=True)
        )
        top = jnp.maximum(top, jnp.max(far, axis=-1, keepdims=True))
        near = jnp.exp2((near - top) * factor)
        prev = jnp.exp2((prev - top) * factor)
        far = jnp.exp2((far - top) * factor)
        total = jnp.sum(near, axis=-1, keepdims=True) + jnp.sum(prev, axis=-1, keepdims=True)
        total += jnp.sum(far, axis=-1, keepdims=True)
        mixed = dot(near, kv_own[i, 1]) + dot(prev, kv_prev[i, 1]) + dot(far, kv_far[i, 1])
        o_buf[:, at] = (mixed / total).astype(jnp.bfloat16)

    def far_here(i, n):
        @pl.when(row > 1)
        def _():
            to_far(i, n).wait_recv()

    lane = lax.broadcasted_iota(jnp.int32, (tokens, HEAD_DIM), 1)

    def add_gap(i):
        for g in range(group):
            mine = o_buf[:, head_cols(i, g)].astype(jnp.float32)
            theirs = other[i - half, :, g * HEAD_DIM:(g + 1) * HEAD_DIM].astype(jnp.float32)
            policy = jnp.where(mp == 0, mine, theirs)
            apart = mine - theirs
            here = lane == (i - half) * group + g
            gap_num[...] = jnp.where(
                here, jnp.sum(apart * apart, axis=-1, keepdims=True), gap_num[...]
            )
            gap_den[...] = jnp.where(
                here, jnp.sum(policy * policy, axis=-1, keepdims=True), gap_den[...]
            )

    last = kv_local - 1
    for i in range(last):
        if i == last - 1:
            for g in range(group):
                near_part(last, g)
        for n in range(2):
            far_here(i, n)
        for g in range(group):
            one_head(i, g)
        local_o(i).start()
        if i < half:
            to_mate(i).start()
        else:
            to_mate(i - half).wait_recv()
            add_gap(i)
    to_mate(last - half).wait_recv()
    far_here(last, 0)
    for g in range(group):
        far_part(last, g)
    far_here(last, 1)
    for g in range(group):
        last_part(last, g)
    local_o(last).start()
    add_gap(last)
    num = jnp.transpose(gap_num[...])[: half * group] / HEAD_DIM
    den = jnp.transpose(gap_den[...])[: half * group] / HEAD_DIM
    gap_out[...] = num / (den + 1e-06)

    for i in range(kv_local):
        local_o(i).wait()
        if i < half:
            to_mate(i).wait_send()
        for n in range(2):
            @pl.when(row < rows - 1)
            def _():
                to_prev(i, n).wait_send()

            @pl.when((row > 0) & (row < rows - 1))
            def _():
                to_far(i, n).wait_send()


def fused(rows, queries, keys, values, lengths):
    tokens = queries.shape[1]
    kv_local = keys.shape[2] // HEAD_DIM
    group = HEADS // KV_HEADS
    width = queries.shape[2]
    half = kv_local // 2
    kv = pltpu.VMEM((kv_local, 2, tokens, HEAD_DIM), jnp.bfloat16)
    dma = pltpu.SemaphoreType.DMA
    return pl.pallas_call(
        functools.partial(kernel, (rows, tokens, kv_local, group)),
        out_shape=(
            jax.ShapeDtypeStruct((1, tokens, width), jnp.bfloat16),
            jax.ShapeDtypeStruct((half * group, tokens), jnp.float32),
        ),
        in_specs=[pl.BlockSpec(memory_space=pltpu.HBM)] * 4,
        out_specs=(pl.BlockSpec(memory_space=pl.ANY), pl.BlockSpec(memory_space=pltpu.VMEM)),
        scratch_shapes=[
            pltpu.SMEM((2,), jnp.int32),
            pltpu.VMEM((tokens, width), jnp.bfloat16),
            kv, kv, kv,
            pltpu.VMEM((tokens, width), jnp.bfloat16),
            pltpu.VMEM((half, tokens, group * HEAD_DIM), jnp.bfloat16),
            pltpu.VMEM((3, tokens, tokens), jnp.float32),
            pltpu.VMEM((tokens, HEAD_DIM), jnp.float32),
            pltpu.VMEM((tokens, HEAD_DIM), jnp.float32),
            pltpu.VMEM((group, tokens, HEAD_DIM), jnp.float32),
            pltpu.VMEM((group, tokens, HEAD_DIM), jnp.float32),
            pltpu.VMEM((group, tokens, HEAD_DIM), jnp.float32),
            pltpu.VMEM((group, tokens, tokens), jnp.bfloat16),
            dma, dma((kv_local,)), dma((kv_local, 2)), dma((kv_local,)),
            dma((kv_local, 2)), dma((kv_local, 2)), dma((kv_local, 2)), dma((kv_local, 2)),
            dma((half,)), dma((half,)),
        ],
        compiler_params=pltpu.CompilerParams(
            collective_id=0, has_side_effects=True, vmem_limit_bytes=48 << 20
        ),
    )(lengths, queries, keys, values)


def solution(mesh):
    in_specs = (
        P("mp", ("groups", "row"), "col"),
        P("mp", ("groups", "row"), "col"),
        P("mp", ("groups", "row"), "col"),
        P("groups"),
    )
    out_specs = (P("mp", ("groups", "row"), "col"), P(("col", "mp"), ("groups", "row")))
    rows = mesh.shape["row"]

    def body(queries, keys, values, lengths):
        if lengths.shape[0] == 2 and rows == 4:
            return fused(rows, queries, keys, values, lengths)
        return per_device(queries, keys, values, lengths)

    return jax.shard_map(
        body, mesh=mesh, in_specs=in_specs, out_specs=out_specs, check_vma=False
    )
```

```python
import functools
import math

import jax
import jax.numpy as jnp
from jax import lax
from jax.experimental import pallas as pl
from jax.experimental.pallas import tpu as pltpu
from jax.sharding import PartitionSpec as P

HEADS = 40
KV_HEADS = 8
HEAD_DIM = 128


def from_behind(block, axis, distance):
    devices = range(lax.axis_size(axis))
    route = [(i - distance, i) for i in devices if i - distance in devices]
    return lax.ppermute(block, axis, route)


def swapped(block, axis, distance):
    count = lax.axis_size(axis)
    route = []
    for low in range(count):
        high = low | 1 << distance
        if high != low and high < count:
            route += [(low, high), (high, low)]
    return lax.ppermute(block, axis, route)


def relative_gap(first, second, tokens_here, heads_count):
    first = first.astype(jnp.float32).reshape(tokens_here, heads_count, HEAD_DIM)
    second = second.astype(jnp.float32).reshape(tokens_here, heads_count, HEAD_DIM)
    difference = first - second
    scale_sum = jnp.mean(first * first, axis=-1) + 1e-06
    return jnp.transpose(jnp.mean(difference * difference, axis=-1) / scale_sum)


def per_device(queries, keys, values, lengths):
    tokens_here = queries.shape[1]
    width_here = keys.shape[2]
    kv_local = width_here // HEAD_DIM
    group_size = HEADS // KV_HEADS
    heads_local = kv_local * group_size
    factor = 1.0 / math.sqrt(HEAD_DIM)
    row_pos = lax.axis_index("row")
    first_pos = row_pos * tokens_here
    query_pos = first_pos + jnp.arange(tokens_here, dtype=jnp.int32)
    finish = jnp.cumsum(lengths)
    begin_at = jnp.sum(
        jnp.where(finish[None, :] <= query_pos[:, None], lengths[None, :], 0), axis=1
    )
    lowest = begin_at[0]
    highest = first_pos + tokens_here - 1
    query_rows = queries[0].reshape(tokens_here, kv_local, group_size, HEAD_DIM)

    def update(running, stacked, offset):
        best, summed, accum = running
        amount = stacked.shape[1]
        key_rows = stacked[0].reshape(amount, kv_local, HEAD_DIM)
        value_rows = stacked[1].reshape(amount, kv_local, HEAD_DIM)
        scores = (
            jnp.einsum("tkgd,nkd->kgtn", query_rows, key_rows, preferred_element_type=jnp.float32)
            * factor
        )
        key_pos = offset + jnp.arange(amount, dtype=jnp.int32)
        allowed = (key_pos[None, :] >= begin_at[:, None]) & (key_pos[None, :] <= query_pos[:, None])
        masked = jnp.where(allowed, scores, -jnp.inf)
        fresh_best = jnp.maximum(best, jnp.max(masked, axis=-1))
        weights = jnp.where(allowed, jnp.exp(masked - fresh_best[..., None]), 0.0)
        shrink = jnp.exp(best - fresh_best)
        summed = summed * shrink + jnp.sum(weights, axis=-1)
        accum = accum * shrink[..., None] + jnp.einsum(
            "kgtn,nkd->kgtd",
            weights.astype(jnp.bfloat16),
            value_rows,
            preferred_element_type=jnp.float32,
        )
        return (fresh_best, summed, accum)

    def absorb(running, stacked, offset):
        amount = stacked.shape[1]
        needed = (offset + amount > lowest) & (offset <= highest)
        return lax.cond(
            needed, lambda inner: update(inner, stacked, offset), lambda inner: inner, running
        )

    start_state = (
        jnp.full((kv_local, group_size, tokens_here), -1e30, jnp.float32),
        jnp.zeros((kv_local, group_size, tokens_here), jnp.float32),
        jnp.zeros((kv_local, group_size, tokens_here, HEAD_DIM), jnp.float32),
    )
    paired = jnp.concatenate([keys, values], axis=0)
    reach = lax.axis_size("row") // 2 + 1
    running = absorb(start_state, paired, first_pos)

    def advance(step_id, loop_state):
        inner, moving = loop_state
        moving = from_behind(moving, "row", 1)
        return (absorb(inner, moving, (row_pos - step_id) * tokens_here), moving)

    running, _ = lax.fori_loop(1, reach + 1, advance, (running, paired))
    best, summed, accum = running
    mixed = accum / summed[..., None]
    outputs = (
        jnp.transpose(mixed, (2, 0, 1, 3))
        .reshape(tokens_here, heads_local * HEAD_DIM)
        .astype(jnp.bfloat16)[None]
    )
    half_heads = heads_local // 2
    partner = swapped(outputs, "mp", 0)
    model_pos = lax.axis_index("mp")
    is_policy = model_pos == 0
    policy = jnp.where(is_policy, outputs[0], partner[0])
    anchor = jnp.where(is_policy, partner[0], outputs[0])
    column_at = model_pos * half_heads * HEAD_DIM
    policy_part = lax.dynamic_slice_in_dim(policy, column_at, half_heads * HEAD_DIM, 1)
    anchor_part = lax.dynamic_slice_in_dim(anchor, column_at, half_heads * HEAD_DIM, 1)
    gap = relative_gap(policy_part, anchor_part, tokens_here, half_heads)
    return (outputs, gap)


MESH = pl.DeviceIdType.MESH
DROP = -1e30


def kernel(sizes, lens_in, q_in, k_in, v_in, o_out, gap_out, lens, q_buf, kv_own, kv_prev, kv_far,
           o_buf, other, bias, gap_num, gap_den, tops, totals, mixes, far_mass, lens_sem, q_sem,
           kv_sem, o_sem, prev_send, prev_recv, far_send, far_recv, mp_send, mp_recv):
    rows, tokens, kv_local, group = sizes
    wide = group * HEAD_DIM
    half = kv_local // 2
    factor = math.log2(math.e) / math.sqrt(HEAD_DIM)
    row = lax.axis_index("row")
    mp = lax.axis_index("mp")
    after = lax.rem(row + 1, rows)
    before = lax.rem(row + rows - 1, rows)

    def head_of(i):
        return lax.rem(i + half * (1 - mp), kv_local)

    def cols(i):
        return pl.ds(pl.multiple_of(head_of(i) * HEAD_DIM, HEAD_DIM), HEAD_DIM)

    def wide_cols(i):
        return pl.ds(pl.multiple_of(head_of(i) * wide, HEAD_DIM), wide)

    def local_kv(i, n):
        src = (k_in, v_in)[n]
        return pltpu.make_async_copy(src.at[0, :, cols(i)], kv_own.at[i, n], kv_sem.at[i, n])

    def local_q(i):
        return pltpu.make_async_copy(
            q_in.at[0, :, wide_cols(i)], q_buf.at[:, wide_cols(i)], q_sem.at[i]
        )

    def local_o(i):
        return pltpu.make_async_copy(
            o_buf.at[:, wide_cols(i)], o_out.at[0, :, wide_cols(i)], o_sem.at[i]
        )

    def to_prev(i, n):
        src = (k_in, v_in)[n]
        return pltpu.make_async_remote_copy(
            src_ref=src.at[0, :, cols(i)], dst_ref=kv_prev.at[i, n],
            send_sem=prev_send.at[i, n], recv_sem=prev_recv.at[i, n],
            device_id={"row": after}, device_id_type=MESH,
        )

    def to_far(i, n):
        return pltpu.make_async_remote_copy(
            src_ref=kv_prev.at[i, n], dst_ref=kv_far.at[i, n],
            send_sem=far_send.at[i, n], recv_sem=far_recv.at[i, n],
            device_id={"row": after}, device_id_type=MESH,
        )

    def to_mate(i):
        return pltpu.make_async_remote_copy(
            src_ref=o_buf.at[:, wide_cols(i)], dst_ref=other.at[i],
            send_sem=mp_send.at[i], recv_sem=mp_recv.at[i],
            device_id={"mp": 1 - mp}, device_id_type=MESH,
        )

    lens_copy = pltpu.make_async_copy(lens_in, lens, lens_sem)
    lens_copy.start()
    for i in range(kv_local):
        for n in range(2):
            local_kv(i, n).start()
        local_q(i).start()
    barrier = pltpu.get_barrier_semaphore()
    for neighbour in (after, before):
        pl.semaphore_signal(barrier, inc=1, device_id={"row": neighbour}, device_id_type=MESH)
    pl.semaphore_signal(barrier, inc=1, device_id={"mp": 1 - mp}, device_id_type=MESH)
    pl.semaphore_wait(barrier, 3)

    @pl.when(row < rows - 1)
    def _():
        for i in range(kv_local):
            for n in range(2):
                to_prev(i, n).start()

    @pl.when(row == 0)
    def _():
        kv_prev[...] = jnp.zeros_like(kv_prev)

    @pl.when(row < 2)
    def _():
        kv_far[...] = jnp.zeros_like(kv_far)

    lens_copy.wait()
    first, second = lens[0], lens[1]
    qi = lax.broadcasted_iota(jnp.int32, (tokens, tokens), 0) + row * tokens
    ki = lax.broadcasted_iota(jnp.int32, (tokens, tokens), 1) + row * tokens
    begin = jnp.where(first <= qi, first, 0) + jnp.where(first + second <= qi, second, 0)
    bias[0] = jnp.where((ki >= begin) & (ki <= qi), 0.0, DROP)
    bias[1] = jnp.where(ki - tokens >= begin, 0.0, DROP)
    bias[2] = jnp.where(ki - 2 * tokens >= begin, 0.0, DROP)
    gap_num[...] = jnp.zeros_like(gap_num)
    gap_den[...] = jnp.zeros_like(gap_den)
    for i in range(kv_local):
        local_q(i).wait()
        for n in range(2):
            local_kv(i, n).wait()

    @pl.when(row > 0)
    def _():
        for i in range(kv_local):
            for n in range(2):
                to_prev(i, n).wait_recv()

                @pl.when(row < rows - 1)
                def _():
                    to_far(i, n).start()

    def dot_t(a, b):
        return lax.dot_general(a, b, (((1,), (1,)), ((), ())), preferred_element_type=jnp.float32)

    def dot(a, b):
        return jnp.dot(a.astype(jnp.bfloat16), b, preferred_element_type=jnp.float32)

    def head_cols(i, g):
        at = head_of(i) * wide + g * HEAD_DIM
        return pl.ds(pl.multiple_of(at, HEAD_DIM), HEAD_DIM)

    def near_part(i, g):
        q = q_buf[:, head_cols(i, g)]
        own = dot_t(q, kv_own[i, 0]) + bias[0]
        prev = dot_t(q, kv_prev[i, 0]) + bias[1]
        top = jnp.maximum(
            jnp.max(own, axis=-1, keepdims=True), jnp.max(prev, axis=-1, keepdims=True)
        )
        own = jnp.exp2((own - top) * factor)
        prev = jnp.exp2((prev - top) * factor)
        total = jnp.sum(own, axis=-1, keepdims=True) + jnp.sum(prev, axis=-1, keepdims=True)
        tops[g] = jnp.broadcast_to(top, (tokens, HEAD_DIM))
        totals[g] = jnp.broadcast_to(total, (tokens, HEAD_DIM))
        mixes[g] = dot(own, kv_own[i, 1]) + dot(prev, kv_prev[i, 1])

    def far_part(i, g):
        q = q_buf[:, head_cols(i, g)]
        far = dot_t(q, kv_far[i, 0]) + bias[2]
        old = tops[g][:, :1]
        top = jnp.maximum(old, jnp.max(far, axis=-1, keepdims=True))
        far = jnp.exp2((far - top) * factor)
        shrink = jnp.exp2((old - top) * factor)
        total = totals[g][:, :1] * shrink + jnp.sum(far, axis=-1, keepdims=True)
        totals[g] = jnp.broadcast_to(1.0 / total, (tokens, HEAD_DIM))
        mixes[g] = mixes[g] * shrink
        far_mass[g] = far.astype(jnp.bfloat16)

    def last_part(i, g):
        mixed = mixes[g] + dot(far_mass[g], kv_far[i, 1])
        o_buf[:, head_cols(i, g)] = (mixed * totals[g]).astype(jnp.bfloat16)

    def one_head(i, g):
        at = head_cols(i, g)
        q = q_buf[:, at]
        near = dot_t(q, kv_own[i, 0]) + bias[0]
        prev = dot_t(q, kv_prev[i, 0]) + bias[1]
        far = dot_t(q, kv_far[i, 0]) + bias[2]
        top = jnp.maximum(
            jnp.max(near, axis=-1, keepdims=True), jnp.max(prev, axis=-1, keepdims=True)
        )
        top = jnp.maximum(top, jnp.max(far, axis=-1, keepdims=True))
        near = jnp.exp2((near - top) * factor)
        prev = jnp.exp2((prev - top) * factor)
        far = jnp.exp2((far - top) * factor)
        total = jnp.sum(near, axis=-1, keepdims=True) + jnp.sum(prev, axis=-1, keepdims=True)
        total += jnp.sum(far, axis=-1, keepdims=True)
        mixed = dot(near, kv_own[i, 1]) + dot(prev, kv_prev[i, 1]) + dot(far, kv_far[i, 1])
        o_buf[:, at] = (mixed / total).astype(jnp.bfloat16)

    def far_here(i, n):
        @pl.when(row > 1)
        def _():
            to_far(i, n).wait_recv()

    lane = lax.broadcasted_iota(jnp.int32, (tokens, HEAD_DIM), 1)

    def add_gap(i):
        for g in range(group):
            mine = o_buf[:, head_cols(i, g)].astype(jnp.float32)
            theirs = other[i - half, :, g * HEAD_DIM:(g + 1) * HEAD_DIM].astype(jnp.float32)
            policy = jnp.where(mp == 0, mine, theirs)
            apart = mine - theirs
            here = lane == (i - half) * group + g
            gap_num[...] = jnp.where(
                here, jnp.sum(apart * apart, axis=-1, keepdims=True), gap_num[...]
            )
            gap_den[...] = jnp.where(
                here, jnp.sum(policy * policy, axis=-1, keepdims=True), gap_den[...]
            )

    last = kv_local - 1
    for i in range(last):
        if i == last - 1:
            for g in range(group):
                near_part(last, g)
        for n in range(2):
            far_here(i, n)
        for g in range(group):
            one_head(i, g)
        local_o(i).start()
        if i < half:
            to_mate(i).start()
        else:
            to_mate(i - half).wait_recv()
            add_gap(i)
    to_mate(last - half).wait_recv()
    far_here(last, 0)
    for g in range(group):
        far_part(last, g)
    far_here(last, 1)
    for g in range(group):
        last_part(last, g)
    local_o(last).start()
    add_gap(last)
    num = jnp.transpose(gap_num[...])[: half * group] / HEAD_DIM
    den = jnp.transpose(gap_den[...])[: half * group] / HEAD_DIM
    gap_out[...] = num / (den + 1e-06)

    for i in range(kv_local):
        local_o(i).wait()
        if i < half:
            to_mate(i).wait_send()
        for n in range(2):
            @pl.when(row < rows - 1)
            def _():
                to_prev(i, n).wait_send()

            @pl.when((row > 0) & (row < rows - 1))
            def _():
                to_far(i, n).wait_send()


def fused(rows, queries, keys, values, lengths):
    tokens = queries.shape[1]
    kv_local = keys.shape[2] // HEAD_DIM
    group = HEADS // KV_HEADS
    width = queries.shape[2]
    half = kv_local // 2
    kv = pltpu.VMEM((kv_local, 2, tokens, HEAD_DIM), jnp.bfloat16)
    dma = pltpu.SemaphoreType.DMA
    return pl.pallas_call(
        functools.partial(kernel, (rows, tokens, kv_local, group)),
        out_shape=(
            jax.ShapeDtypeStruct((1, tokens, width), jnp.bfloat16),
            jax.ShapeDtypeStruct((half * group, tokens), jnp.float32),
        ),
        in_specs=[pl.BlockSpec(memory_space=pltpu.HBM)] * 4,
        out_specs=(pl.BlockSpec(memory_space=pl.ANY), pl.BlockSpec(memory_space=pltpu.VMEM)),
        scratch_shapes=[
            pltpu.SMEM((2,), jnp.int32),
            pltpu.VMEM((tokens, width), jnp.bfloat16),
            kv, kv, kv,
            pltpu.VMEM((tokens, width), jnp.bfloat16),
            pltpu.VMEM((half, tokens, group * HEAD_DIM), jnp.bfloat16),
            pltpu.VMEM((3, tokens, tokens), jnp.float32),
            pltpu.VMEM((tokens, HEAD_DIM), jnp.float32),
            pltpu.VMEM((tokens, HEAD_DIM), jnp.float32),
            pltpu.VMEM((group, tokens, HEAD_DIM), jnp.float32),
            pltpu.VMEM((group, tokens, HEAD_DIM), jnp.float32),
            pltpu.VMEM((group, tokens, HEAD_DIM), jnp.float32),
            pltpu.VMEM((group, tokens, tokens), jnp.bfloat16),
            dma, dma((kv_local,)), dma((kv_local, 2)), dma((kv_local,)),
            dma((kv_local, 2)), dma((kv_local, 2)), dma((kv_local, 2)), dma((kv_local, 2)),
            dma((half,)), dma((half,)),
        ],
        compiler_params=pltpu.CompilerParams(
            collective_id=0, has_side_effects=True, vmem_limit_bytes=67043328
        ),
    )(lengths, queries, keys, values)


def solution(mesh):
    in_specs = (
        P("mp", ("groups", "row"), "col"),
        P("mp", ("groups", "row"), "col"),
        P("mp", ("groups", "row"), "col"),
        P("groups"),
    )
    out_specs = (P("mp", ("groups", "row"), "col"), P(("col", "mp"), ("groups", "row")))
    rows = mesh.shape["row"]

    def body(queries, keys, values, lengths):
        if lengths.shape[0] == 2 and rows == 4:
            return fused(rows, queries, keys, values, lengths)
        return per_device(queries, keys, values, lengths)

    return jax.shard_map(
        body, mesh=mesh, in_specs=in_specs, out_specs=out_specs, check_vma=False
    )
```
